32 devices in a mesh: dp: 8 (over y, x, core), tensor: 4 (over z).
Axes of the slice: x: 2, y: 2, z: 4, core: 2. Of those that a mesh axis runs over, the one named last changes fastest.
Arguments:
- block_input_rows: bfloat16 [2048, 2048], P('dp'), may hold values from -6 to 6
- initial_embedding: bfloat16 [2048, 2048], P('dp'), may hold values from -6 to 6
- document_index_rows: int32 [8, 256], P('dp'), may hold values from 0 to 7, as said below
- positions: int32 [8, 256], P('dp'), may hold values from 0 to 1023, as said below
- cotangent: bfloat16 [2048, 2048], P('dp'), may hold values from -6 to 6
- attention_norm_gain: float32 [4096], replicated, may hold values from 0.5 to 1.5
- query_key_value_weight: bfloat16 [3, 4096, 4096], P(None, 'dp', 'tensor'), may hold values from -0.09375 to 0.09375
- adapter_attention_down: bfloat16 [4096, 384], P('dp'), may hold values from -0.09375 to 0.09375
- adapter_attention_up: bfloat16 [3, 128, 4096], P(None, 'dp', 'tensor'), may hold values from -0.5 to 0.5
- attention_output_weight: bfloat16 [4096, 4096], P('tensor', 'dp'), may hold values from -0.375 to 0.375
- feedfwd_norm_gain: float32 [4096], replicated, may hold values from 0.5 to 1.5
- gate_up_weight: bfloat16 [2, 4096, 8192], P(None, 'dp', 'tensor'), may hold values from -0.09375 to 0.09375
- adapter_feedfwd_down: bfloat16 [4096, 128], P('dp'), may hold values from -0.09375 to 0.09375
- adapter_feedfwd_up: bfloat16 [2, 128, 8192], P(None, 'dp', 'tensor'), may hold values from -0.5 to 0.5
- feedfwd_down_weight: bfloat16 [8192, 4096], P('tensor', 'dp'), may hold values from -0.0625 to 0.0625
- attention_linear_weight: bfloat16 [4096, 2048], P('dp'), may hold values from -0.09375 to 0.09375
- mixer_norm_gain: float32 [2048], replicated, may hold values from 0.5 to 1.5
- mixer_input_gate_signal_weight: bfloat16 [2, 2048, 4096], P(None, 'dp', 'tensor'), may hold values from -0.125 to 0.125
- mixer_input_bc_weight: bfloat16 [2048, 256], P('dp'), may hold values from -0.125 to 0.125
- mixer_input_stepsize_weight: bfloat16 [2048, 64], P('dp', 'tensor'), may hold values from -0.125 to 0.125
- convolve_signal_taps: float32 [4, 4096], P(None, 'tensor'), may hold values from -0.8 to 0.8
- convolve_bc_taps: float32 [4, 256], replicated, may hold values from -0.8 to 0.8
- log_decay_rate: float32 [64], P('tensor'), may hold values from -6 to -1
- stepsize_bias: float32 [64], P('tensor'), may hold values from -3 to 0.5
- direct_path_weight: float32 [64], P('tensor'), may hold values from 0.5 to 1.5
- gated_norm_gain: float32 [4096], P('tensor'), may hold values from 0.5 to 1.5
- mixer_output_weight: bfloat16 [4096, 2048], P('tensor', 'dp'), may hold values from -0.09375 to 0.09375
Outputs:
- hidden_out: bfloat16 [2048, 2048], P('dp')
- grad_hidden_in: bfloat16 [2048, 2048], P('dp')
- grad_embed_in: bfloat16 [2048, 2048], P('dp')
- grad_norm_attn_gain: float32 [4096], replicated
- grad_w_qkv: float32 [3, 4096, 4096], P(None, 'dp', 'tensor')
- grad_lora_attn_down: float32 [4096, 384], P('dp')
- grad_lora_attn_up: float32 [3, 128, 4096], P(None, 'dp', 'tensor')
- grad_w_attn_out: float32 [4096, 4096], P('tensor', 'dp')
- grad_norm_mlp_gain: float32 [4096], replicated
- grad_w_gate_up: float32 [2, 4096, 8192], P(None, 'dp', 'tensor')
- grad_lora_mlp_down: float32 [4096, 128], P('dp')
- grad_lora_mlp_up: float32 [2, 128, 8192], P(None, 'dp', 'tensor')
- grad_w_mlp_down: float32 [8192, 4096], P('tensor', 'dp')
- grad_w_linear: float32 [4096, 2048], P('dp')
- grad_norm_mamba_gain: float32 [2048], replicated
- grad_w_in_zx: float32 [2, 2048, 4096], P(None, 'dp', 'tensor')
- grad_w_in_bc: float32 [2048, 256], P('dp')
- grad_w_in_dt: float32 [2048, 64], P('dp', 'tensor')
- gradient_convolve_signal: float32 [4, 4096], P(None, 'tensor')
- gradient_convolve_bc: float32 [4, 256], replicated
- gradient_log_decay: float32 [64], P('tensor')
- gradient_stepsize_bias: float32 [64], P('tensor')
- gradient_direct_weight: float32 [64], P('tensor')
- gradient_gated_norm_gain: float32 [4096], P('tensor')
- grad_w_out_mamba: float32 [4096, 2048], P('tensor', 'dp')
The draws below stay inside these ranges and needn't reach their ends.
Inputs may be any that keep to these rules, and one draw needn't show every extreme that they name: `document_index_rows`: in each packed sequence the ids start at 0 at its first token, never fall, rise by one where a document starts, and end at 7. `positions`: A token's position is its index inside its document plus an offset of that document; the first document of every packed sequence has offset 0, and the last token of every packed sequence has position 1023.
All inputs are finite; a program needn't handle non-finite values.
Results may differ from the reference program's by a relative error of at most 0.033.
Values may be sent and summed in bfloat16 or wider, within the bound.
No kernel may reach another device: no remote copies, remote signals or barrier semaphores. Data moves between devices by JAX's collectives and lax.ppermute only.
A program may use at most 640 MiB of HBM per device.

```python
import math
import jax
import jax.numpy as jnp
from jax import lax

D = 2048
ATTN_INPUT_WIDTH = 4096
HEAD_DIM = 128
HEADS_BY_SIZE = 4096
ADAPTER_RANK = 128
FEEDFWD_UNITS = 8192
MHEADS = 64
DI = 4096
STATE = 128
CONV = 4
SEQ = 256
DOCS = 8
SEQS = 8
TOKENS = 2048


def doc_layout(key):
    cut_key = jax.random.fold_in(key, 101)
    offset_key = jax.random.fold_in(key, 202)
    row_keys = jax.random.split(cut_key, SEQS)
    cuts = jax.vmap(lambda row_key: jax.random.permutation(row_key, SEQ - 1)[:DOCS - 1].astype(jnp.int32) + 1)(row_keys)
    token_index = jnp.arange(SEQ, dtype=jnp.int32)
    passed = cuts[:, :, None] <= token_index[None, None, :]
    segment = jnp.sum(passed.astype(jnp.int32), axis=1)
    start_row = jnp.max(jnp.where(passed, cuts[:, :, None], 0), axis=1)
    last_start = jnp.max(cuts, axis=1)
    last_length = SEQ - last_start
    offsets = jax.random.randint(offset_key, (SEQS, DOCS), 0, 3 * SEQ, dtype=jnp.int32)
    doc_index = jnp.arange(DOCS, dtype=jnp.int32)[None, :]
    offsets = jnp.where(doc_index == DOCS - 1, (4 * SEQ - last_length)[:, None], offsets)
    offsets = jnp.where(doc_index == 0, 0, offsets)
    position = token_index[None, :] - start_row + jnp.take_along_axis(offsets, segment, axis=1)
    return (segment.astype(jnp.int32), position.astype(jnp.int32))


def draw_document_index_rows(key, part):
    return doc_layout(key)[0]


def draw_positions(key, part):
    return doc_layout(key)[1]


def block_scale(own_key, extent, pieces, least, top_value):
    loudness = 1.0
    for axis_at, blocks in pieces:
        steps = jax.random.uniform(jax.random.fold_in(jax.random.fold_in(own_key, 6), axis_at), (blocks,), jnp.float32, least / len(pieces), top_value / len(pieces))
        loudness = loudness * jnp.repeat(jnp.exp(steps), extent[axis_at] // blocks).reshape((-1,) + (1,) * (len(extent) - 1 - axis_at))
    return loudness


def centred(own_key, dims, width, bound, cuts=(), kind=jnp.bfloat16):
    loudness = block_scale(own_key, dims, cuts, -0.22, 0.18) if cuts else 1.0
    array = jax.random.normal(own_key, dims, jnp.float32) * width * loudness
    return jnp.minimum(jnp.maximum(array, -bound), bound).astype(kind)


def setup_inputs(seed: int = 0) -> dict:
    key_of = jax.random.split(jax.random.key(seed), 28)
    block_input_rows = centred(key_of[0], (TOKENS, D), 1.0, 6.0, ((0, 8),))
    initial_embedding = centred(key_of[1], (TOKENS, D), 1.0, 6.0, ((0, 8),))
    document_index_rows = draw_document_index_rows(jax.random.fold_in(key_of[27], 71), 0)
    positions = draw_positions(jax.random.fold_in(key_of[27], 71), 0)
    cotangent = centred(key_of[4], (TOKENS, D), 1.0, 6.0, ((0, 8),))
    attention_norm_gain = jnp.clip(1.0 + 0.1 * jax.random.normal(key_of[5], (ATTN_INPUT_WIDTH,), jnp.float32), 0.5, 1.5)
    query_key_value_weight = centred(key_of[6], (3, ATTN_INPUT_WIDTH, HEADS_BY_SIZE), ATTN_INPUT_WIDTH ** -0.5, 0.09375, ((1, 8), (2, 4)))
    adapter_attention_down = centred(key_of[7], (ATTN_INPUT_WIDTH, 3 * ADAPTER_RANK), ATTN_INPUT_WIDTH ** -0.5, 0.09375, ((0, 8),))
    adapter_attention_up = centred(key_of[8], (3, ADAPTER_RANK, HEADS_BY_SIZE), ADAPTER_RANK ** -0.5, 0.5, ((1, 8), (2, 4)))
    attention_output_weight = centred(key_of[9], (HEADS_BY_SIZE, ATTN_INPUT_WIDTH), (HEADS_BY_SIZE // 16) ** -0.5, 0.375, ((0, 4), (1, 8)))
    feedfwd_norm_gain = jnp.clip(1.0 + 0.1 * jax.random.normal(key_of[10], (ATTN_INPUT_WIDTH,), jnp.float32), 0.5, 1.5)
    gate_up_weight = centred(key_of[11], (2, ATTN_INPUT_WIDTH, FEEDFWD_UNITS), ATTN_INPUT_WIDTH ** -0.5, 0.09375, ((1, 8), (2, 4)))
    adapter_feedfwd_down = centred(key_of[12], (ATTN_INPUT_WIDTH, ADAPTER_RANK), ATTN_INPUT_WIDTH ** -0.5, 0.09375, ((0, 8),))
    adapter_feedfwd_up = centred(key_of[13], (2, ADAPTER_RANK, FEEDFWD_UNITS), ADAPTER_RANK ** -0.5, 0.5, ((1, 8), (2, 4)))
    feedfwd_down_weight = centred(key_of[14], (FEEDFWD_UNITS, ATTN_INPUT_WIDTH), FEEDFWD_UNITS ** -0.5, 0.0625, ((0, 4), (1, 8)))
    attention_linear_weight = centred(key_of[15], (ATTN_INPUT_WIDTH, D), ATTN_INPUT_WIDTH ** -0.5, 0.09375, ((0, 8),))
    mixer_norm_gain = jnp.clip(1.0 + 0.1 * jax.random.normal(key_of[16], (D,), jnp.float32), 0.5, 1.5)
    mixer_input_gate_signal_weight = centred(key_of[17], (2, D, DI), D ** -0.5, 0.125, ((1, 8), (2, 4)))
    mixer_input_bc_weight = centred(key_of[18], (D, 2 * STATE), D ** -0.5, 0.125, ((0, 8),))
    mixer_input_stepsize_weight = centred(key_of[19], (D, MHEADS), D ** -0.5, 0.125, ((0, 8), (1, 4)))
    convolve_signal_taps = jnp.clip(jax.random.uniform(key_of[20], (CONV, DI), jnp.float32, -0.8, 0.8) * block_scale(key_of[20], (CONV, DI), ((1, 4),), -0.4, 0.0), -0.8, 0.8)
    convolve_bc_taps = jnp.clip(jax.random.uniform(key_of[21], (CONV, 2 * STATE), jnp.float32, -0.8, 0.8), -0.8, 0.8)
    log_decay_rate = jnp.clip(-6.0 + 5.0 * jax.random.uniform(key_of[22], (MHEADS,), jnp.float32) ** block_scale(key_of[22], (MHEADS,), ((0, 4),), -0.2, 0.2), -6.0, -1.0)
    stepsize_bias = jnp.clip(-3.0 + 3.5 * jax.random.uniform(key_of[23], (MHEADS,), jnp.float32) ** block_scale(key_of[23], (MHEADS,), ((0, 4),), -0.2, 0.2), -3.0, 0.5)
    direct_path_weight = jnp.clip(0.5 + 1.0 * jax.random.uniform(key_of[24], (MHEADS,), jnp.float32) ** block_scale(key_of[24], (MHEADS,), ((0, 4),), -0.2, 0.2), 0.5, 1.5)
    gated_norm_gain = jnp.clip(1.0 + 0.1 * jax.random.normal(key_of[25], (DI,), jnp.float32), 0.5, 1.5)
    mixer_output_weight = centred(key_of[26], (DI, D), DI ** -0.5, 0.09375, ((0, 4), (1, 8)))
    return {"block_input_rows": block_input_rows, "initial_embedding": initial_embedding, "document_index_rows": document_index_rows, "positions": positions, "cotangent": cotangent, "attention_norm_gain": attention_norm_gain, "query_key_value_weight": query_key_value_weight, "adapter_attention_down": adapter_attention_down, "adapter_attention_up": adapter_attention_up, "attention_output_weight": attention_output_weight, "feedfwd_norm_gain": feedfwd_norm_gain, "gate_up_weight": gate_up_weight, "adapter_feedfwd_down": adapter_feedfwd_down, "adapter_feedfwd_up": adapter_feedfwd_up, "feedfwd_down_weight": feedfwd_down_weight, "attention_linear_weight": attention_linear_weight, "mixer_norm_gain": mixer_norm_gain, "mixer_input_gate_signal_weight": mixer_input_gate_signal_weight, "mixer_input_bc_weight": mixer_input_bc_weight, "mixer_input_stepsize_weight": mixer_input_stepsize_weight, "convolve_signal_taps": convolve_signal_taps, "convolve_bc_taps": convolve_bc_taps, "log_decay_rate": log_decay_rate, "stepsize_bias": stepsize_bias, "direct_path_weight": direct_path_weight, "gated_norm_gain": gated_norm_gain, "mixer_output_weight": mixer_output_weight}


norm_eps = 1e-05
rope_base = 10000.0

def matrix_product_f32(left_op, right_op):
    return jnp.dot(left_op, right_op, preferred_element_type=jnp.float32)

def rms_rate(values):
    return lax.rsqrt(lax.optimization_barrier(jnp.mean(values * values, axis=-1, keepdims=True)) + norm_eps)

def norm_back(values, row_rate, gain_vec, upstream):
    scaled = upstream * gain_vec
    inner_mean = lax.optimization_barrier(jnp.mean(scaled * values, axis=-1, keepdims=True))
    grad_values = row_rate * scaled - values * row_rate * row_rate * row_rate * inner_mean
    grad_gain = lax.optimization_barrier(jnp.sum(upstream * values * row_rate, axis=0))
    return (grad_values, grad_gain)

def rope_tables(positions, head_width):
    half_width = head_width // 2
    frequency = rope_base ** (-jnp.arange(half_width, dtype=jnp.float32) / half_width)
    angles = positions.astype(jnp.float32)[:, None] * frequency[None, :]
    return (jnp.cos(angles), jnp.sin(angles))

def rotate(values, cos_table, sin_table, inverse):
    half_width = values.shape[-1] // 2
    first_half = values[..., :half_width]
    second_half = values[..., half_width:]
    cos_rows = cos_table[:, None, :]
    sin_rows = sin_table[:, None, :]
    if inverse:
        sin_rows = -sin_rows
    return jnp.concatenate([first_half * cos_rows - second_half * sin_rows, second_half * cos_rows + first_half * sin_rows], axis=-1)

def seq_mask(segment):
    token_index = jnp.arange(segment.shape[0])
    return (token_index[None, :] <= token_index[:, None]) & (segment[None, :] == segment[:, None])

def attend_forward(packed):
    query_b, key_b, value_b, segment = packed
    scale_factor = query_b.shape[-1] ** (-0.5)
    scores = jnp.einsum('thd,shd->hts', query_b.astype(jnp.float32), key_b.astype(jnp.float32)) * scale_factor
    allowed = seq_mask(segment)[None, :, :]
    scores = jnp.where(allowed, scores, -1e+30)
    top_score = lax.optimization_barrier(jnp.max(scores, axis=-1, keepdims=True))
    exp_scores = jnp.exp(scores - top_score)
    row_total = lax.optimization_barrier(jnp.sum(exp_scores, axis=-1, keepdims=True))
    probs_b = (exp_scores / row_total).astype(jnp.bfloat16)
    output = jnp.einsum('hts,shd->thd', probs_b.astype(jnp.float32), value_b.astype(jnp.float32))
    return (output, (top_score + jnp.log(row_total))[:, :, 0])

def attend_backward(packed):
    query_b, key_b, value_b, segment, out_b, log_total, grad_b = packed
    scale_factor = query_b.shape[-1] ** (-0.5)
    query_f = query_b.astype(jnp.float32)
    key_f = key_b.astype(jnp.float32)
    grad_f = grad_b.astype(jnp.float32)
    scores = jnp.einsum('thd,shd->hts', query_f, key_f) * scale_factor
    allowed = seq_mask(segment)[None, :, :]
    probs = jnp.where(allowed, jnp.exp(scores - log_total[:, :, None]), 0.0)
    probs_b = probs.astype(jnp.bfloat16)
    grad_value = jnp.einsum('hts,thd->shd', probs_b.astype(jnp.float32), grad_f)
    grad_probs = jnp.einsum('thd,shd->hts', grad_f, value_b.astype(jnp.float32))
    delta_rows = lax.optimization_barrier(jnp.sum(grad_f * out_b.astype(jnp.float32), axis=-1))
    grad_scores = probs * (grad_probs - delta_rows.T[:, :, None])
    scores_b = grad_scores.astype(jnp.bfloat16).astype(jnp.float32)
    grad_query = jnp.einsum('hts,shd->thd', scores_b, key_f) * scale_factor
    grad_key = jnp.einsum('hts,thd->shd', scores_b, query_f) * scale_factor
    return (grad_query, grad_key, grad_value)

def causal_conv(signal, conv_taps, segment):
    length = signal.shape[0]
    tap_count = conv_taps.shape[0]
    result = jnp.zeros_like(signal)
    segment = segment.astype(jnp.int32)
    for tap_index in range(tap_count):
        delay_rows = tap_count - 1 - tap_index
        if delay_rows == 0:
            result = result + conv_taps[tap_index][None, :] * signal
        else:
            shifted = jnp.concatenate([jnp.zeros((delay_rows, signal.shape[1]), signal.dtype), signal[:length - delay_rows]], axis=0)
            earlier = jnp.concatenate([jnp.full((delay_rows,), -1, jnp.int32), segment[:length - delay_rows]], axis=0)
            keep_rows = earlier == segment
            result = result + conv_taps[tap_index][None, :] * jnp.where(keep_rows[:, None], shifted, 0.0)
    return result

def bc_mix(bc_in, conv_taps, segment):
    return jax.nn.silu(causal_conv(bc_in, conv_taps, segment))

def mixer_core(x_pre, gate_z, bc_post, step_raw, conv_taps, log_decay_rate, stepsize_bias, direct_path_weight, segment):
    length = x_pre.shape[0]
    heads_here = step_raw.shape[-1]
    x_act = jax.nn.silu(causal_conv(x_pre, conv_taps, segment))
    state_size = bc_post.shape[-1] // 2
    b_mat = bc_post[:, :state_size]
    c_mat = bc_post[:, state_size:]
    step_size = jax.nn.softplus(step_raw + stepsize_bias[None, :])
    log_decay = step_size * (-jnp.exp(log_decay_rate))[None, :]
    cumulative = jnp.cumsum(log_decay, axis=0).T
    gram_mat = jnp.dot(c_mat, b_mat.T, precision=lax.Precision.HIGHEST)
    allowed = seq_mask(segment)[None, :, :]
    spread = cumulative[:, :, None] - cumulative[:, None, :]
    decay_mat = jnp.where(allowed, jnp.exp(jnp.where(allowed, spread, 0.0)), 0.0)
    weights_mix = decay_mat * gram_mat[None, :, :] * step_size.T[:, None, :]
    x_heads = x_act.reshape(length, heads_here, -1)
    mixed_heads = jnp.einsum('hts,shp->thp', weights_mix, x_heads, precision=lax.Precision.HIGHEST) + direct_path_weight[None, :, None] * x_heads
    return mixed_heads.reshape(length, -1) * jax.nn.silu(gate_z)

def mixer_pullback(packed, conv_taps, log_decay_rate, stepsize_bias, direct_path_weight):
    x_seq, z_seq, bc_seq, step_seq, segment, upstream = packed

    def forward_map(x_in, z_in, bc_val, step_in, taps_in, decay_in, bias_in, skip_in):
        return mixer_core(x_in, z_in, bc_val, step_in, taps_in, decay_in, bias_in, skip_in, segment)
    primal_out, pullback = jax.vjp(forward_map, x_seq, z_seq, bc_seq, step_seq, conv_taps, log_decay_rate, stepsize_bias, direct_path_weight)
    return pullback(upstream)

def bc_pullback(packed, conv_taps):
    bc_seq, segment, upstream = packed
    primal_out, pullback = jax.vjp(lambda bc_val, taps_val: bc_mix(bc_val, taps_val, segment), bc_seq, conv_taps)
    return pullback(upstream)

def by_seq(array_in, seq_count):
    return array_in.reshape(seq_count, -1, array_in.shape[-1])

def block_pass(weight_sequence, hidden_blk, embed_blk, segment_blk, position_blk, cotangent_blk):
    attention_norm_gain, query_key_value_weight, adapter_attention_down, adapter_attention_up, attention_output_weight, feedfwd_norm_gain, gate_up_weight, adapter_feedfwd_down, adapter_feedfwd_up, feedfwd_down_weight, attention_linear_weight, mixer_norm_gain, mixer_input_gate_signal_weight, mixer_input_bc_weight, mixer_input_stepsize_weight, convolve_signal_taps, convolve_bc_taps, log_decay_rate, stepsize_bias, direct_path_weight, gated_norm_gain, mixer_output_weight = weight_sequence
    seq_count, seq_len = segment_blk.shape
    row_count = seq_count * seq_len
    model_width = hidden_blk.shape[1]
    adapter_rank_size = adapter_attention_up.shape[1]
    head_shape = (seq_count, seq_len, -1, HEAD_DIM)
    joined = jnp.concatenate([hidden_blk.astype(jnp.float32), embed_blk.astype(jnp.float32)], axis=1)
    rate_one = rms_rate(joined)
    first_normalized = (joined * rate_one * attention_norm_gain).astype(jnp.bfloat16)
    lowrank_attention = matrix_product_f32(first_normalized, adapter_attention_down).astype(jnp.bfloat16)
    projected_rows = [matrix_product_f32(first_normalized, query_key_value_weight[member_entry]) + matrix_product_f32(lowrank_attention[:, member_entry * adapter_rank_size:(member_entry + 1) * adapter_rank_size], adapter_attention_up[member_entry]) for member_entry in range(3)]
    cos_table, sin_table = rope_tables(position_blk.reshape(-1), HEAD_DIM)
    query_b = rotate(projected_rows[0].reshape(row_count, -1, HEAD_DIM), cos_table, sin_table, False).astype(jnp.bfloat16)
    key_b = rotate(projected_rows[1].reshape(row_count, -1, HEAD_DIM), cos_table, sin_table, False).astype(jnp.bfloat16)
    value_b = projected_rows[2].reshape(row_count, -1, HEAD_DIM).astype(jnp.bfloat16)
    query_seq = query_b.reshape(head_shape)
    key_seq = key_b.reshape(head_shape)
    value_seq = value_b.reshape(head_shape)
    attended_f, log_total = lax.map(attend_forward, (query_seq, key_seq, value_seq, segment_blk))
    attended = attended_f.astype(jnp.bfloat16)
    attended_rows = attended.reshape(row_count, -1)
    attn_total = matrix_product_f32(attended_rows, attention_output_weight)
    after_attn = joined + attn_total
    rate_two = rms_rate(after_attn)
    second_normalized = (after_attn * rate_two * feedfwd_norm_gain).astype(jnp.bfloat16)
    lowrank_feedfwd = matrix_product_f32(second_normalized, adapter_feedfwd_down).astype(jnp.bfloat16)
    gate_before_act = matrix_product_f32(second_normalized, gate_up_weight[0]) + matrix_product_f32(lowrank_feedfwd, adapter_feedfwd_up[0])
    up_before_act = matrix_product_f32(second_normalized, gate_up_weight[1]) + matrix_product_f32(lowrank_feedfwd, adapter_feedfwd_up[1])
    act_value, gelu_pullback = jax.vjp(lambda gate_val, up_val: jax.nn.gelu(gate_val, approximate=False) * up_val, gate_before_act, up_before_act)
    mlp_act = act_value.astype(jnp.bfloat16)
    after_mlp = after_attn + matrix_product_f32(mlp_act, feedfwd_down_weight)
    after_mlp_b = after_mlp.astype(jnp.bfloat16)
    bridge = hidden_blk.astype(jnp.float32) + matrix_product_f32(after_mlp_b, attention_linear_weight)
    rate_three = rms_rate(bridge)
    normed_three = (bridge * rate_three * mixer_norm_gain).astype(jnp.bfloat16)
    gate_z = matrix_product_f32(normed_three, mixer_input_gate_signal_weight[0])
    x_pre = matrix_product_f32(normed_three, mixer_input_gate_signal_weight[1])
    bc_in = matrix_product_f32(normed_three, mixer_input_bc_weight)
    step_raw = matrix_product_f32(normed_three, mixer_input_stepsize_weight)
    bc_post = lax.map(lambda packed: bc_mix(packed[0], convolve_bc_taps, packed[1]), (by_seq(bc_in, seq_count), segment_blk))
    mixed_seq = lax.map(lambda packed: mixer_core(packed[0], packed[1], packed[2], packed[3], convolve_signal_taps, log_decay_rate, stepsize_bias, direct_path_weight, packed[4]), (by_seq(x_pre, seq_count), by_seq(gate_z, seq_count), bc_post, by_seq(step_raw, seq_count), segment_blk))
    mixed_out = mixed_seq.reshape(row_count, -1)
    gate_rate = lax.rsqrt(lax.optimization_barrier(jnp.mean(mixed_out * mixed_out, axis=-1, keepdims=True)) + norm_eps)
    normed_mix = (mixed_out * gate_rate * gated_norm_gain).astype(jnp.bfloat16)
    mamba_total = matrix_product_f32(normed_mix, mixer_output_weight)
    hidden_out = (bridge + mamba_total).astype(jnp.bfloat16)
    grad_top = cotangent_blk.astype(jnp.float32)
    gradient_mixer_output_weight = matrix_product_f32(normed_mix.T, cotangent_blk)
    grad_normed_mix = matrix_product_f32(cotangent_blk, mixer_output_weight.T)
    weighted = grad_normed_mix * gated_norm_gain
    inner_mean = lax.optimization_barrier(jnp.mean(weighted * mixed_out, axis=-1, keepdims=True))
    grad_mixed = gate_rate * weighted - mixed_out * gate_rate * gate_rate * gate_rate * inner_mean
    gradient_gated_norm_gain = lax.optimization_barrier(jnp.sum(grad_normed_mix * mixed_out * gate_rate, axis=0))
    mixer_grads = lax.map(lambda packed: mixer_pullback(packed, convolve_signal_taps, log_decay_rate, stepsize_bias, direct_path_weight), (by_seq(x_pre, seq_count), by_seq(gate_z, seq_count), bc_post, by_seq(step_raw, seq_count), segment_blk, by_seq(grad_mixed, seq_count)))
    grad_x_seq, grad_z_seq, grad_bc_seq, grad_step_seq, conv_terms, decay_terms, bias_terms, skip_terms = mixer_grads
    gradient_convolve_signal = lax.optimization_barrier(jnp.sum(conv_terms, axis=0))
    gradient_log_decay = lax.optimization_barrier(jnp.sum(decay_terms, axis=0))
    gradient_stepsize_bias = lax.optimization_barrier(jnp.sum(bias_terms, axis=0))
    gradient_direct_weight = lax.optimization_barrier(jnp.sum(skip_terms, axis=0))
    grad_z_b = grad_z_seq.reshape(row_count, -1).astype(jnp.bfloat16)
    grad_x_b = grad_x_seq.reshape(row_count, -1).astype(jnp.bfloat16)
    grad_step_b = grad_step_seq.reshape(row_count, -1).astype(jnp.bfloat16)
    bc_grads = lax.map(lambda packed: bc_pullback(packed, convolve_bc_taps), (by_seq(bc_in, seq_count), segment_blk, grad_bc_seq))
    grad_bc_in = bc_grads[0].reshape(row_count, -1)
    gradient_convolve_bc = lax.optimization_barrier(jnp.sum(bc_grads[1], axis=0))
    grad_bc_b = grad_bc_in.astype(jnp.bfloat16)
    gradient_input_gate_signal = jnp.stack([matrix_product_f32(normed_three.T, grad_z_b), matrix_product_f32(normed_three.T, grad_x_b)])
    gradient_input_bc = matrix_product_f32(normed_three.T, grad_bc_b)
    gradient_input_stepsize = matrix_product_f32(normed_three.T, grad_step_b)
    grad_normed_three = matrix_product_f32(grad_z_b, mixer_input_gate_signal_weight[0].T) + matrix_product_f32(grad_x_b, mixer_input_gate_signal_weight[1].T) + matrix_product_f32(grad_step_b, mixer_input_stepsize_weight.T) + matrix_product_f32(grad_bc_b, mixer_input_bc_weight.T)
    back_three, gradient_third_gain = norm_back(bridge, rate_three, mixer_norm_gain, grad_normed_three)
    grad_bridge = grad_top + back_three
    grad_bridge_b = grad_bridge.astype(jnp.bfloat16)
    gradient_output_linear = matrix_product_f32(after_mlp_b.T, grad_bridge_b)
    grad_after_mlp = matrix_product_f32(grad_bridge_b, attention_linear_weight.T)
    grad_mlp_b = grad_after_mlp.astype(jnp.bfloat16)
    gradient_feedfwd_down = matrix_product_f32(mlp_act.T, grad_mlp_b)
    grad_act = matrix_product_f32(grad_mlp_b, feedfwd_down_weight.T)
    grad_gate, grad_up = gelu_pullback(grad_act)
    gradient_couple = [grad_gate.astype(jnp.bfloat16), grad_up.astype(jnp.bfloat16)]
    gradient_gate_up_weight = jnp.stack([matrix_product_f32(second_normalized.T, gradient_couple[member_entry]) for member_entry in range(2)])
    gradient_feedfwd_up_adapter = jnp.stack([matrix_product_f32(lowrank_feedfwd.T, gradient_couple[member_entry]) for member_entry in range(2)])
    gradient_lowrank_feedfwd = (matrix_product_f32(gradient_couple[0], adapter_feedfwd_up[0].T) + matrix_product_f32(gradient_couple[1], adapter_feedfwd_up[1].T)).astype(jnp.bfloat16)
    gradient_feedfwd_down_adapter = matrix_product_f32(second_normalized.T, gradient_lowrank_feedfwd)
    gradient_second_normalized = matrix_product_f32(gradient_couple[0], gate_up_weight[0].T) + matrix_product_f32(gradient_couple[1], gate_up_weight[1].T) + matrix_product_f32(gradient_lowrank_feedfwd, adapter_feedfwd_down.T)
    back_two, gradient_second_gain = norm_back(after_attn, rate_two, feedfwd_norm_gain, gradient_second_normalized)
    grad_after_attn = grad_after_mlp + back_two
    grad_attn_b = grad_after_attn.astype(jnp.bfloat16)
    gradient_attention_output = matrix_product_f32(attended_rows.T, grad_attn_b)
    grad_attended = matrix_product_f32(grad_attn_b, attention_output_weight.T).astype(jnp.bfloat16)
    grad_query, grad_key, grad_value = lax.map(attend_backward, (query_seq, key_seq, value_seq, segment_blk, attended, log_total, grad_attended.reshape(head_shape)))
    gradient_projected_rows = [rotate(grad_query.reshape(row_count, -1, HEAD_DIM), cos_table, sin_table, True).reshape(row_count, -1).astype(jnp.bfloat16), rotate(grad_key.reshape(row_count, -1, HEAD_DIM), cos_table, sin_table, True).reshape(row_count, -1).astype(jnp.bfloat16), grad_value.reshape(row_count, -1).astype(jnp.bfloat16)]
    gradient_query_key_value = jnp.stack([matrix_product_f32(first_normalized.T, gradient_projected_rows[member_entry]) for member_entry in range(3)])
    gradient_attention_up = jnp.stack([matrix_product_f32(lowrank_attention[:, member_entry * adapter_rank_size:(member_entry + 1) * adapter_rank_size].T, gradient_projected_rows[member_entry]) for member_entry in range(3)])
    gradient_lowrank_attention = jnp.concatenate([matrix_product_f32(gradient_projected_rows[member_entry], adapter_attention_up[member_entry].T) for member_entry in range(3)], axis=1).astype(jnp.bfloat16)
    gradient_attention_down = matrix_product_f32(first_normalized.T, gradient_lowrank_attention)
    gradient_first_normalized = matrix_product_f32(gradient_projected_rows[0], query_key_value_weight[0].T) + matrix_product_f32(gradient_projected_rows[1], query_key_value_weight[1].T) + matrix_product_f32(gradient_projected_rows[2], query_key_value_weight[2].T) + matrix_product_f32(gradient_lowrank_attention, adapter_attention_down.T)
    back_one, gradient_first_gain = norm_back(joined, rate_one, attention_norm_gain, gradient_first_normalized)
    grad_joined = grad_after_attn + back_one
    grad_hidden = (grad_bridge + grad_joined[:, :model_width]).astype(jnp.bfloat16)
    grad_embed = grad_joined[:, model_width:].astype(jnp.bfloat16)
    gradient_collection = (gradient_first_gain, gradient_query_key_value, gradient_attention_down, gradient_attention_up, gradient_attention_output, gradient_second_gain, gradient_gate_up_weight, gradient_feedfwd_down_adapter, gradient_feedfwd_up_adapter, gradient_feedfwd_down, gradient_output_linear, gradient_third_gain, gradient_input_gate_signal, gradient_input_bc, gradient_input_stepsize, gradient_convolve_signal, gradient_convolve_bc, gradient_log_decay, gradient_stepsize_bias, gradient_direct_weight, gradient_gated_norm_gain, gradient_mixer_output_weight)
    return ((hidden_out, grad_hidden, grad_embed), gradient_collection)

def reference(block_input_rows, initial_embedding, document_index_rows, positions, cotangent, attention_norm_gain, query_key_value_weight, adapter_attention_down, adapter_attention_up, attention_output_weight, feedfwd_norm_gain, gate_up_weight, adapter_feedfwd_down, adapter_feedfwd_up, feedfwd_down_weight, attention_linear_weight, mixer_norm_gain, mixer_input_gate_signal_weight, mixer_input_bc_weight, mixer_input_stepsize_weight, convolve_signal_taps, convolve_bc_taps, log_decay_rate, stepsize_bias, direct_path_weight, gated_norm_gain, mixer_output_weight):
    weight_sequence = (attention_norm_gain, query_key_value_weight, adapter_attention_down, adapter_attention_up, attention_output_weight, feedfwd_norm_gain, gate_up_weight, adapter_feedfwd_down, adapter_feedfwd_up, feedfwd_down_weight, attention_linear_weight, mixer_norm_gain, mixer_input_gate_signal_weight, mixer_input_bc_weight, mixer_input_stepsize_weight, convolve_signal_taps, convolve_bc_taps, log_decay_rate, stepsize_bias, direct_path_weight, gated_norm_gain, mixer_output_weight)
    block_seqs = math.gcd(SEQS, 8)
    block_count = SEQS // block_seqs
    block_rows = block_seqs * SEQ
    model_width = block_input_rows.shape[1]
    inputs = (block_input_rows.reshape(block_count, block_rows, model_width), initial_embedding.reshape(block_count, block_rows, model_width), document_index_rows.reshape(block_count, block_seqs, SEQ), positions.reshape(block_count, block_seqs, SEQ), cotangent.reshape(block_count, block_rows, model_width))

    def step_fn(grad_carry, blocks):
        outputs, gradient_collection = block_pass(weight_sequence, blocks[0], blocks[1], blocks[2], blocks[3], blocks[4])
        return (tuple((carried + fresh.astype(carried.dtype) for carried, fresh in zip(grad_carry, gradient_collection))), outputs)
    start_carry = tuple((jnp.zeros(weight_item.shape, jnp.float32) for weight_item in weight_sequence))
    totals, outputs = lax.scan(step_fn, start_carry, inputs)
    hidden_out = outputs[0].reshape(-1, model_width)
    grad_hidden = outputs[1].reshape(-1, model_width)
    grad_embed = outputs[2].reshape(-1, model_width)
    return (hidden_out, grad_hidden, grad_embed, totals[0], totals[1], totals[2], totals[3], totals[4], totals[5], totals[6], totals[7], totals[8], totals[9], totals[10], totals[11], totals[12], totals[13], totals[14], totals[15], totals[16], totals[17], totals[18], totals[19], totals[20], totals[21])
```

```python
import jax
import jax.numpy as jnp
from jax import lax
from jax.sharding import PartitionSpec as P

HEAD_DIM = 128


norm_eps = 1e-05
rope_base = 10000.0


def matrix_product_f32(left_op, right_op):
    return jnp.dot(left_op, right_op, preferred_element_type=jnp.float32)


def rms_rate(values):
    return lax.rsqrt(jnp.mean(values * values, axis=-1, keepdims=True) + norm_eps)


def norm_back(values, row_rate, gain_vec, upstream):
    scaled = upstream * gain_vec
    inner_mean = jnp.mean(scaled * values, axis=-1, keepdims=True)
    grad_values = row_rate * scaled - values * row_rate * row_rate * row_rate * inner_mean
    grad_gain = jnp.sum(upstream * values * row_rate, axis=0)
    return (grad_values, grad_gain)


def rope_tables(positions, head_width):
    half_width = head_width // 2
    frequency = rope_base ** (-jnp.arange(half_width, dtype=jnp.float32) / half_width)
    angles = positions.astype(jnp.float32)[:, None] * frequency[None, :]
    return (jnp.cos(angles), jnp.sin(angles))


def rotate(values, cos_table, sin_table, inverse):
    half_width = values.shape[-1] // 2
    first_half = values[..., :half_width]
    second_half = values[..., half_width:]
    cos_rows = cos_table[:, None, :]
    sin_rows = sin_table[:, None, :]
    if inverse:
        sin_rows = -sin_rows
    return jnp.concatenate(
        [
            first_half * cos_rows - second_half * sin_rows,
            second_half * cos_rows + first_half * sin_rows,
        ],
        axis=-1,
    )


def seq_mask(segment):
    token_index = jnp.arange(segment.shape[0])
    return (token_index[None, :] <= token_index[:, None]) & (segment[None, :] == segment[:, None])


def attend_forward(packed):
    query_b, key_b, value_b, segment = packed
    scale_factor = query_b.shape[-1] ** (-0.5)
    scores = (
        jnp.einsum("thd,shd->hts", query_b, key_b, preferred_element_type=jnp.float32)
        * scale_factor
    )
    allowed = seq_mask(segment)[None, :, :]
    scores = jnp.where(allowed, scores, -1e30)
    top_score = jnp.max(scores, axis=-1, keepdims=True)
    exp_scores = jnp.exp(scores - top_score)
    row_total = jnp.sum(exp_scores, axis=-1, keepdims=True)
    probs_b = (exp_scores / row_total).astype(jnp.bfloat16)
    output = jnp.einsum("hts,shd->thd", probs_b, value_b, preferred_element_type=jnp.float32)
    return (output, (top_score + jnp.log(row_total))[:, :, 0])


def attend_backward(packed):
    query_b, key_b, value_b, segment, out_b, log_total, grad_b = packed
    scale_factor = query_b.shape[-1] ** (-0.5)
    scores = (
        jnp.einsum("thd,shd->hts", query_b, key_b, preferred_element_type=jnp.float32)
        * scale_factor
    )
    allowed = seq_mask(segment)[None, :, :]
    probs = jnp.where(allowed, jnp.exp(scores - log_total[:, :, None]), 0.0)
    probs_b = probs.astype(jnp.bfloat16)
    grad_value = jnp.einsum("hts,thd->shd", probs_b, grad_b, preferred_element_type=jnp.float32)
    grad_probs = jnp.einsum("thd,shd->hts", grad_b, value_b, preferred_element_type=jnp.float32)
    delta_rows = jnp.sum(grad_b.astype(jnp.float32) * out_b.astype(jnp.float32), axis=-1)
    grad_scores = probs * (grad_probs - delta_rows.T[:, :, None])
    scores_b = grad_scores.astype(jnp.bfloat16)
    grad_query = (
        jnp.einsum("hts,shd->thd", scores_b, key_b, preferred_element_type=jnp.float32)
        * scale_factor
    )
    grad_key = (
        jnp.einsum("hts,thd->shd", scores_b, query_b, preferred_element_type=jnp.float32)
        * scale_factor
    )
    return (grad_query, grad_key, grad_value)


def causal_conv(signal, conv_taps, segment):
    length = signal.shape[0]
    tap_count = conv_taps.shape[0]
    result = jnp.zeros_like(signal)
    for tap_index in range(tap_count):
        delay_rows = tap_count - 1 - tap_index
        if delay_rows == 0:
            result = result + conv_taps[tap_index][None, :] * signal
        else:
            shifted = jnp.concatenate(
                [
                    jnp.zeros((delay_rows, signal.shape[1]), signal.dtype),
                    signal[: length - delay_rows],
                ],
                axis=0,
            )
            earlier = jnp.concatenate(
                [jnp.full((delay_rows,), -1, jnp.int32), segment[: length - delay_rows]], axis=0
            )
            keep_rows = earlier == segment
            result = result + conv_taps[tap_index][None, :] * jnp.where(
                keep_rows[:, None], shifted, 0.0
            )
    return result


def bc_mix(bc_in, conv_taps, segment):
    return jax.nn.silu(causal_conv(bc_in, conv_taps, segment))


def mixer_core(
    x_pre,
    gate_z,
    bc_post,
    step_raw,
    conv_taps,
    log_decay_rate,
    stepsize_bias,
    direct_path_weight,
    segment,
):
    length = x_pre.shape[0]
    heads_here = step_raw.shape[-1]
    x_act = jax.nn.silu(causal_conv(x_pre, conv_taps, segment))
    state_size = bc_post.shape[-1] // 2
    b_mat = bc_post[:, :state_size]
    c_mat = bc_post[:, state_size:]
    step_size = jax.nn.softplus(step_raw + stepsize_bias[None, :])
    log_decay = step_size * (-jnp.exp(log_decay_rate))[None, :]
    cumulative = jnp.cumsum(log_decay, axis=0).T
    gram_mat = jnp.dot(c_mat, b_mat.T, precision=lax.Precision.HIGHEST)
    allowed = seq_mask(segment)[None, :, :]
    spread = cumulative[:, :, None] - cumulative[:, None, :]
    decay_mat = jnp.where(allowed, jnp.exp(jnp.where(allowed, spread, 0.0)), 0.0)
    weights_mix = decay_mat * gram_mat[None, :, :] * step_size.T[:, None, :]
    x_heads = x_act.reshape(length, heads_here, -1)
    mixed_heads = (
        jnp.einsum("hts,shp->thp", weights_mix, x_heads, precision=lax.Precision.HIGHEST)
        + direct_path_weight[None, :, None] * x_heads
    )
    return mixed_heads.reshape(length, -1) * jax.nn.silu(gate_z)


def mixer_pullback(packed, conv_taps, log_decay_rate, stepsize_bias, direct_path_weight):
    x_seq, z_seq, bc_seq, step_seq, segment, upstream = packed

    def forward_map(x_in, z_in, bc_val, step_in, taps_in, decay_in, bias_in, skip_in):
        return mixer_core(x_in, z_in, bc_val, step_in, taps_in, decay_in, bias_in, skip_in, segment)

    primal_out, pullback = jax.vjp(
        forward_map,
        x_seq,
        z_seq,
        bc_seq,
        step_seq,
        conv_taps,
        log_decay_rate,
        stepsize_bias,
        direct_path_weight,
    )
    return pullback(upstream)


def bc_pullback(packed, conv_taps):
    bc_seq, segment, upstream = packed
    primal_out, pullback = jax.vjp(
        lambda bc_val, taps_val: bc_mix(bc_val, taps_val, segment), bc_seq, conv_taps
    )
    return pullback(upstream)


def by_seq(array_in, seq_count):
    return array_in.reshape(seq_count, -1, array_in.shape[-1])


def flip(axis_name, offset):
    return [(i, i ^ offset) for i in range(lax.axis_size(axis_name))]


def swap(values, axis_name, offset):
    return lax.ppermute(values, axis_name, flip(axis_name, offset))


def axis_bits(axis_name):
    size = lax.axis_size(axis_name)
    bits = []
    step = 1
    while step < size:
        bits.append(step)
        step *= 2
    return bits


def scatter_bits(parity):
    bits = axis_bits("dp")
    rest = bits[1:]
    return bits[:1] + (rest if parity == 0 else rest[::-1])


def block_order(parity):
    order = [0]
    for bit in scatter_bits(parity)[::-1]:
        order = order + [entry | bit for entry in order]
    return order


def reorder(blocks, from_parity, to_parity):
    if from_parity == to_parity:
        return blocks
    have = block_order(from_parity)
    want = block_order(to_parity)
    if have == want:
        return blocks
    return jnp.concatenate([blocks[have.index(k)][None] for k in want], axis=0)


def block_dot(blocks, weight):
    return lax.dot_general(
        blocks, weight, (((blocks.ndim - 1,), (0,)), ((), ())), preferred_element_type=jnp.float32
    )


def dot_scatter(blocks, weight, parity):
    bits = scatter_bits(parity)
    half = blocks.shape[0] // 2
    leaving = block_dot(blocks[half:], weight).astype(jnp.bfloat16)
    arrived = swap(leaving, "dp", bits[0])
    kept = block_dot(blocks[:half], weight) + arrived.astype(jnp.float32)
    for bit in bits[1:]:
        kept = kept.astype(jnp.bfloat16)
        half = kept.shape[0] // 2
        arrived = swap(kept[half:], "dp", bit)
        kept = kept[:half].astype(jnp.float32) + arrived.astype(jnp.float32)
    return kept[0]


def gather_blocks(own, parity):
    blocks = own[None]
    for bit in scatter_bits(parity)[::-1]:
        blocks = jnp.concatenate([blocks, swap(blocks, "dp", bit)], axis=0)
    return blocks


def spread_columns(values, width_axis):
    size = lax.axis_size("dp")
    here = lax.axis_index("dp")
    width = values.shape[width_axis] // size
    blocks = []
    for k in block_order(0):
        part = lax.dynamic_slice_in_dim(values, (here ^ k) * width, width, width_axis)
        blocks.append(part if k == 0 else swap(part, "dp", k))
    return blocks


def sum_blocks_dp(rows):
    order = block_order(0)
    for bit in axis_bits("dp"):
        arrived = swap(rows, "dp", bit)
        rows = rows + jnp.stack([arrived[order.index(k ^ bit)] for k in order])
    return rows


def sum_doubling(values, axis_name):
    for bit in axis_bits(axis_name):
        values = values + swap(values, axis_name, bit)
    return values


def sum_doubling_b(values, axis_name):
    for bit in axis_bits(axis_name):
        mine = values.astype(jnp.bfloat16)
        values = mine.astype(jnp.float32) + swap(mine, axis_name, bit).astype(jnp.float32)
    return values


def tensor_chunk(values, offset):
    rows = values.shape[0] // lax.axis_size("tensor")
    return lax.dynamic_slice_in_dim(values, (lax.axis_index("tensor") ^ offset) * rows, rows, 0)


def tensor_chunks(values):
    return [tensor_chunk(values, j) for j in range(lax.axis_size("tensor"))]


def tensor_join(parts):
    together = jnp.concatenate(parts, axis=0)
    return jnp.concatenate(tensor_chunks(together), axis=0)


def tensor_gather(own):
    return [own if j == 0 else swap(own, "tensor", j) for j in range(lax.axis_size("tensor"))]


def tensor_collect(parts):
    total = parts[0]
    for j in range(1, len(parts)):
        total = total + swap(parts[j].astype(jnp.bfloat16), "tensor", j).astype(jnp.float32)
    return total


def flat_tokens(chunks):
    return jnp.concatenate([c.reshape(-1, c.shape[-1]) for c in chunks], axis=0)


def token_product(left, right):
    return lax.dot_general(
        left, right, (((0,), (0,)), ((), ())), preferred_element_type=jnp.float32
    )


def per_device(
    block_input_rows,
    initial_embedding,
    document_index_rows,
    positions,
    cotangent,
    attention_norm_gain,
    query_key_value_weight,
    adapter_attention_down,
    adapter_attention_up,
    attention_output_weight,
    feedfwd_norm_gain,
    gate_up_weight,
    adapter_feedfwd_down,
    adapter_feedfwd_up,
    feedfwd_down_weight,
    attention_linear_weight,
    mixer_norm_gain,
    mixer_input_gate_signal_weight,
    mixer_input_bc_weight,
    mixer_input_stepsize_weight,
    convolve_signal_taps,
    convolve_bc_taps,
    log_decay_rate,
    stepsize_bias,
    direct_path_weight,
    gated_norm_gain,
    mixer_output_weight,
):
    bf16 = jnp.bfloat16
    f32 = jnp.float32
    in_zx_full = lax.all_gather(mixer_input_gate_signal_weight, "dp", axis=1, tiled=True)
    attention_up_map = lax.all_gather(adapter_attention_up, "dp", axis=1, tiled=True)
    feedfwd_up_adapter = lax.all_gather(adapter_feedfwd_up, "dp", axis=1, tiled=True)
    in_bc_full = lax.all_gather(mixer_input_bc_weight, "dp", axis=0, tiled=True)
    in_dt_full = lax.all_gather(mixer_input_stepsize_weight, "dp", axis=0, tiled=True)
    out_mamba_full = lax.all_gather(mixer_output_weight, "dp", axis=1, tiled=True)

    data_size = lax.axis_size("dp")
    data_here = lax.axis_index("dp")
    ranks = lax.axis_size("tensor")
    seq_count, seq_len = document_index_rows.shape
    row_count = seq_count * seq_len
    chunk_rows = row_count // ranks
    model_width = block_input_rows.shape[1]
    joined_width = 2 * model_width
    share = joined_width // data_size
    rank_size = attention_up_map.shape[1]
    heads_width = query_key_value_weight.shape[2]
    units = gate_up_weight.shape[2]
    mixer_width = in_zx_full.shape[2] * ranks
    head_shape = (seq_count, seq_len, -1, HEAD_DIM)
    parities = [j % 2 for j in range(ranks)]

    joined_b = jnp.concatenate([block_input_rows, initial_embedding], axis=1)
    joined = joined_b.astype(f32)
    rate_one = rms_rate(joined)
    first_normalized = (joined * rate_one * attention_norm_gain).astype(bf16)
    first_blocks = spread_columns(jnp.concatenate(tensor_chunks(first_normalized), axis=0), 1)
    order0 = block_order(0)

    def chunk_of(blocks, j):
        return jnp.stack(
            [
                blocks[order0.index(k)][j * chunk_rows : (j + 1) * chunk_rows]
                for k in block_order(parities[j])
            ]
        )

    first_chunks = [chunk_of(first_blocks, j) for j in range(ranks)]
    qkv_wide = jnp.concatenate(
        [query_key_value_weight[m] for m in range(3)] + [adapter_attention_down], axis=1
    )
    joined_chunk_b = tensor_chunk(joined_b, 0)
    joined_share = jnp.stack(spread_columns(joined_chunk_b, 1)).astype(f32)
    projected = tensor_join(
        [dot_scatter(first_chunks[j], qkv_wide, parities[j]) for j in range(ranks)]
    )
    lowrank_attention = projected[:, 3 * heads_width :].astype(bf16)
    projected_rows = [
        projected[:, m * heads_width : (m + 1) * heads_width]
        + matrix_product_f32(
            lowrank_attention[:, m * rank_size : (m + 1) * rank_size], attention_up_map[m]
        )
        for m in range(3)
    ]
    low_attn_blocks = [
        b.reshape(row_count, -1)
        for b in spread_columns(
            jnp.concatenate(tensor_chunks(lowrank_attention), axis=0).reshape(
                row_count, 3, rank_size
            ),
            2,
        )
    ]
    low_attn_share = flat_tokens([chunk_of(low_attn_blocks, j) for j in range(ranks)])
    cos_table, sin_table = rope_tables(positions.reshape(-1), HEAD_DIM)
    query_b = rotate(
        projected_rows[0].reshape(row_count, -1, HEAD_DIM), cos_table, sin_table, False
    ).astype(bf16)
    key_b = rotate(
        projected_rows[1].reshape(row_count, -1, HEAD_DIM), cos_table, sin_table, False
    ).astype(bf16)
    value_b = projected_rows[2].reshape(row_count, -1, HEAD_DIM).astype(bf16)
    query_seq = query_b.reshape(head_shape)
    key_seq = key_b.reshape(head_shape)
    value_seq = value_b.reshape(head_shape)
    attended_f, log_total = lax.map(
        attend_forward, (query_seq, key_seq, value_seq, document_index_rows)
    )
    attended = attended_f.astype(bf16)
    attended_rows = attended.reshape(row_count, -1)
    attended_chunks = [
        gather_blocks(tensor_chunk(attended_rows, j), parities[j]) for j in range(ranks)
    ]
    after_attn = joined_share + tensor_collect(
        [
            reorder(block_dot(attended_chunks[j], attention_output_weight), parities[j], 0)
            for j in range(ranks)
        ]
    )

    gain_two = lax.dynamic_slice_in_dim(feedfwd_norm_gain, data_here * share, share, 0)
    square_two = sum_blocks_dp(jnp.sum(after_attn * after_attn, axis=-1))
    rate_two = lax.rsqrt(square_two / joined_width + norm_eps)[:, :, None]
    rate_two_chunks = tensor_gather(rate_two[0])
    second_own = (after_attn * gain_two).astype(bf16)
    second_chunks = [
        reorder(part, 0, parities[j]) for j, part in enumerate(tensor_gather(second_own))
    ]
    gate_up_wide = jnp.concatenate(
        [gate_up_weight[0], gate_up_weight[1], adapter_feedfwd_down], axis=1
    )

    def gated(gate_val, up_val):
        return jax.nn.gelu(gate_val, approximate=False) * up_val

    gate_chunks, up_chunks, low_chunks, low_raw, act_chunks, mlp_parts = [], [], [], [], [], []
    for j in range(ranks):
        wide = dot_scatter(second_chunks[j], gate_up_wide, parities[j])
        low_raw.append(wide[:, 2 * units :].astype(bf16))
        low = (wide[:, 2 * units :] * rate_two_chunks[j]).astype(bf16)
        gate_pre = wide[:, :units] * rate_two_chunks[j] + matrix_product_f32(
            low, feedfwd_up_adapter[0]
        )
        up_pre = wide[:, units : 2 * units] * rate_two_chunks[j] + matrix_product_f32(
            low, feedfwd_up_adapter[1]
        )
        act = gather_blocks(gated(gate_pre, up_pre).astype(bf16), parities[j])
        gate_chunks.append(gate_pre)
        up_chunks.append(up_pre)
        act_chunks.append(act)
        mlp_parts.append(reorder(block_dot(act, feedfwd_down_weight), parities[j], 0))
    low_feed_blocks = spread_columns(jnp.concatenate(low_raw, axis=0), 1)
    low_feed_share = flat_tokens([chunk_of(low_feed_blocks, j) for j in range(ranks)])
    after_mlp_b = (after_attn + tensor_collect(mlp_parts)).astype(bf16)

    column_half = model_width // 2
    bridge = tensor_chunk(block_input_rows, 0).astype(f32) + jnp.concatenate(
        [
            dot_scatter(
                reorder(after_mlp_b, 0, p),
                attention_linear_weight[:, p * column_half : (p + 1) * column_half],
                p,
            )
            for p in range(2)
        ],
        axis=1,
    )
    rate_three = rms_rate(bridge)
    normed_three = tensor_join(
        tensor_gather((bridge * rate_three * mixer_norm_gain).astype(bf16))
    )
    gate_z = matrix_product_f32(normed_three, in_zx_full[0])
    x_pre = matrix_product_f32(normed_three, in_zx_full[1])
    bc_in = matrix_product_f32(normed_three, in_bc_full)
    step_raw = matrix_product_f32(normed_three, in_dt_full)
    bc_post = lax.map(
        lambda packed: bc_mix(packed[0], convolve_bc_taps, packed[1]),
        (by_seq(bc_in, seq_count), document_index_rows),
    )
    mixed_seq = lax.map(
        lambda packed: mixer_core(
            packed[0],
            packed[1],
            packed[2],
            packed[3],
            convolve_signal_taps,
            log_decay_rate,
            stepsize_bias,
            direct_path_weight,
            packed[4],
        ),
        (
            by_seq(x_pre, seq_count),
            by_seq(gate_z, seq_count),
            bc_post,
            by_seq(step_raw, seq_count),
            document_index_rows,
        ),
    )
    mixed_out = mixed_seq.reshape(row_count, -1)
    grad_normed_mix = matrix_product_f32(cotangent, out_mamba_full.T)
    weighted = grad_normed_mix * gated_norm_gain
    square_sum, inner_sum = sum_doubling(
        jnp.stack(
            [jnp.sum(mixed_out * mixed_out, axis=-1), jnp.sum(weighted * mixed_out, axis=-1)]
        ),
        "tensor",
    )[:, :, None]
    gate_rate = lax.rsqrt(square_sum / mixer_width + norm_eps)
    normed_mix = (mixed_out * gate_rate * gated_norm_gain).astype(bf16)
    mamba_part = matrix_product_f32(normed_mix, out_mamba_full)
    hidden_chunk = (bridge + tensor_collect(tensor_chunks(mamba_part))).astype(bf16)
    hidden_out = tensor_join(tensor_gather(hidden_chunk))
    gradient_mixer_output_weight = matrix_product_f32(normed_mix.T, cotangent)
    grad_mixed = gate_rate * weighted - mixed_out * gate_rate * gate_rate * gate_rate * (
        inner_sum / mixer_width
    )
    gradient_gated_norm_gain = jnp.sum(grad_normed_mix * mixed_out * gate_rate, axis=0)
    mixer_grads = lax.map(
        lambda packed: mixer_pullback(
            packed, convolve_signal_taps, log_decay_rate, stepsize_bias, direct_path_weight
        ),
        (
            by_seq(x_pre, seq_count),
            by_seq(gate_z, seq_count),
            bc_post,
            by_seq(step_raw, seq_count),
            document_index_rows,
            by_seq(grad_mixed, seq_count),
        ),
    )
    (
        grad_x_seq,
        grad_z_seq,
        grad_bc_seq,
        grad_step_seq,
        conv_terms,
        decay_terms,
        bias_terms,
        skip_terms,
    ) = mixer_grads
    gradient_convolve_signal = jnp.sum(conv_terms, axis=0)
    gradient_log_decay = jnp.sum(decay_terms, axis=0)
    gradient_stepsize_bias = jnp.sum(bias_terms, axis=0)
    gradient_direct_weight = jnp.sum(skip_terms, axis=0)
    grad_z_b = grad_z_seq.reshape(row_count, -1).astype(bf16)
    grad_x_b = grad_x_seq.reshape(row_count, -1).astype(bf16)
    grad_step_b = grad_step_seq.reshape(row_count, -1).astype(bf16)
    partial_in = (
        matrix_product_f32(grad_z_b, in_zx_full[0].T)
        + matrix_product_f32(grad_x_b, in_zx_full[1].T)
        + matrix_product_f32(grad_step_b, in_dt_full.T)
    )
    sum_in = tensor_collect(tensor_chunks(partial_in))
    sum_bc = sum_doubling_b(grad_bc_seq.reshape(row_count, -1), "tensor")
    bc_grads = lax.map(
        lambda packed: bc_pullback(packed, convolve_bc_taps),
        (by_seq(bc_in, seq_count), document_index_rows, by_seq(sum_bc, seq_count)),
    )
    grad_bc_b = bc_grads[0].reshape(row_count, -1).astype(bf16)
    gradient_convolve_bc = jnp.sum(bc_grads[1], axis=0)
    grad_normed_three = sum_in + matrix_product_f32(tensor_chunk(grad_bc_b, 0), in_bc_full.T)
    back_three, gradient_third_gain = norm_back(
        bridge, rate_three, mixer_norm_gain, grad_normed_three
    )
    grad_bridge = tensor_chunk(cotangent, 0).astype(f32) + back_three
    grad_bridge_blocks = gather_blocks(grad_bridge.astype(bf16), 0)
    grad_after_mlp = block_dot(grad_bridge_blocks, attention_linear_weight.T)

    grad_mlp_chunks = [
        reorder(part, 0, parities[j])
        for j, part in enumerate(tensor_gather(grad_after_mlp.astype(bf16)))
    ]
    dgu_chunks, two_parts, low_parts = [], [], []
    for j in range(ranks):
        grad_act = dot_scatter(grad_mlp_chunks[j], feedfwd_down_weight.T, parities[j])
        act_primal, gelu_pullback = jax.vjp(gated, gate_chunks[j], up_chunks[j])
        grad_gate, grad_up = gelu_pullback(grad_act)
        low_parts.append(
            matrix_product_f32(grad_gate.astype(bf16), feedfwd_up_adapter[0].T)
            + matrix_product_f32(grad_up.astype(bf16), feedfwd_up_adapter[1].T)
        )
        scaled = jnp.concatenate(
            [
                (grad_gate * rate_two_chunks[j]).astype(bf16),
                (grad_up * rate_two_chunks[j]).astype(bf16),
            ],
            axis=1,
        )
        dgu = gather_blocks(scaled, parities[j])
        dgu_chunks.append(dgu)
        two_parts.append(
            reorder(block_dot(dgu, gate_up_wide[:, : 2 * units].T), parities[j], 0)
        )
    low_back = gather_blocks(
        (tensor_collect(low_parts) * rate_two[0]).astype(bf16), 0
    )
    scaled_two = tensor_collect(two_parts) + block_dot(low_back, adapter_feedfwd_down.T)
    weighted_two = scaled_two * gain_two
    inner_two = sum_blocks_dp(jnp.sum(weighted_two * after_attn, axis=-1))[:, :, None]
    grad_after_attn = (
        grad_after_mlp
        + weighted_two
        - after_attn * rate_two * rate_two * (inner_two / joined_width)
    )
    gain_two_part = jnp.sum(scaled_two * after_attn, axis=(0, 1))
    grad_attn_b = grad_after_attn.astype(bf16)

    grad_attn_chunks = [
        reorder(part, 0, parities[j]) for j, part in enumerate(tensor_gather(grad_attn_b))
    ]
    grad_attended = tensor_join(
        [
            dot_scatter(grad_attn_chunks[j], attention_output_weight.T, parities[j]).astype(bf16)
            for j in range(ranks)
        ]
    )
    grad_query, grad_key, grad_value = lax.map(
        attend_backward,
        (
            query_seq,
            key_seq,
            value_seq,
            document_index_rows,
            attended,
            log_total,
            grad_attended.reshape(head_shape),
        ),
    )
    grad_projected = [
        rotate(grad_query.reshape(row_count, -1, HEAD_DIM), cos_table, sin_table, True)
        .reshape(row_count, -1)
        .astype(bf16),
        rotate(grad_key.reshape(row_count, -1, HEAD_DIM), cos_table, sin_table, True)
        .reshape(row_count, -1)
        .astype(bf16),
        grad_value.reshape(row_count, -1).astype(bf16),
    ]
    grad_projected_rows = jnp.concatenate(grad_projected, axis=1)
    low_attn_part = jnp.concatenate(
        [matrix_product_f32(grad_projected[m], attention_up_map[m].T) for m in range(3)], axis=1
    )
    low_attn_back = gather_blocks(
        tensor_collect(tensor_chunks(low_attn_part)).astype(bf16), 0
    )
    dqkv_chunks, one_parts = [], []
    for j in range(ranks):
        dqkv = gather_blocks(tensor_chunk(grad_projected_rows, j), parities[j])
        dqkv_chunks.append(dqkv)
        one_parts.append(
            reorder(block_dot(dqkv, qkv_wide[:, : 3 * heads_width].T), parities[j], 0)
        )
    grad_first = tensor_collect(one_parts) + block_dot(low_attn_back, adapter_attention_down.T)

    def collect_columns(blocks):
        parts = [
            blocks[i] if k == 0 else swap(blocks[i], "dp", k) for i, k in enumerate(order0)
        ]
        by_offset = jnp.stack([parts[order0.index(k)] for k in range(data_size)])
        return jnp.concatenate(
            [
                lax.dynamic_index_in_dim(by_offset, data_here ^ i, 0, keepdims=False)
                for i in range(data_size)
            ],
            axis=1,
        ).astype(f32)

    grad_after_rows = collect_columns(grad_attn_b)
    grad_first_rows = collect_columns(grad_first.astype(bf16))
    back_one, gain_one_part = norm_back(
        joined_chunk_b.astype(f32),
        tensor_chunk(rate_one, 0),
        attention_norm_gain,
        grad_first_rows,
    )
    grad_joined = grad_after_rows + back_one
    grad_pair = jnp.concatenate(
        [
            (grad_bridge + grad_joined[:, :model_width]).astype(bf16),
            grad_joined[:, model_width:].astype(bf16),
        ],
        axis=1,
    )
    grad_pair_rows = tensor_join(tensor_gather(grad_pair))
    grad_hidden = grad_pair_rows[:, :model_width]
    grad_embed = grad_pair_rows[:, model_width:]

    first_full = flat_tokens(first_chunks)
    dqkv_full = flat_tokens(dqkv_chunks)
    share_qkv = jnp.stack(
        [
            token_product(first_full, dqkv_full[:, m * heads_width : (m + 1) * heads_width])
            for m in range(3)
        ]
    )
    low_width = low_attn_share.shape[1] // 3
    share_attn_up = jnp.stack(
        [
            token_product(
                low_attn_share[:, m * low_width : (m + 1) * low_width],
                dqkv_full[:, m * heads_width : (m + 1) * heads_width],
            )
            for m in range(3)
        ]
    )
    share_attn_down = sum_doubling_b(
        token_product(
            first_chunks[0].reshape(-1, share),
            low_attn_back.reshape(-1, low_attn_back.shape[-1]),
        ),
        "tensor",
    )
    share_attn_out = token_product(flat_tokens(attended_chunks), flat_tokens(grad_attn_chunks))
    second_full = flat_tokens(second_chunks)
    dgu_full = flat_tokens(dgu_chunks)
    share_gate_up = jnp.stack(
        [token_product(second_full, dgu_full[:, m * units : (m + 1) * units]) for m in range(2)]
    )
    shared_feedfwd_up_adapter = jnp.stack(
        [token_product(low_feed_share, dgu_full[:, m * units : (m + 1) * units]) for m in range(2)]
    )
    shared_feedfwd_down_adapter = sum_doubling_b(
        token_product(second_own.reshape(-1, share), low_back.reshape(-1, rank_size)), "tensor"
    )
    share_mlp_down = token_product(flat_tokens(act_chunks), flat_tokens(grad_mlp_chunks))
    linear_part = token_product(
        after_mlp_b.reshape(-1, share), grad_bridge_blocks.reshape(-1, model_width)
    )
    linear_chunk = tensor_collect(tensor_chunks(linear_part)).astype(bf16)
    share_linear = tensor_join(tensor_gather(linear_chunk)).astype(f32)
    gradient_input_gate_signal = jnp.stack(
        [matrix_product_f32(normed_three.T, grad_z_b), matrix_product_f32(normed_three.T, grad_x_b)]
    )
    gradient_input_bc = matrix_product_f32(normed_three.T, grad_bc_b)
    gradient_input_stepsize = matrix_product_f32(normed_three.T, grad_step_b)
    share_out_mamba = lax.psum_scatter(
        gradient_mixer_output_weight.astype(bf16), "dp", scatter_dimension=1, tiled=True
    ).astype(f32)
    share_in_zx = lax.psum_scatter(
        gradient_input_gate_signal.astype(bf16), "dp", scatter_dimension=1, tiled=True
    ).astype(f32)
    share_in_bc = lax.psum_scatter(
        gradient_input_bc.astype(bf16), "dp", scatter_dimension=0, tiled=True
    ).astype(f32)
    share_in_dt = lax.psum_scatter(
        gradient_input_stepsize.astype(bf16), "dp", scatter_dimension=0, tiled=True
    ).astype(f32)

    def pooled(parts, axis_names):
        flat = jnp.concatenate([p.reshape(-1) for p in parts])
        for axis_name in axis_names:
            flat = sum_doubling(flat, axis_name)
        pieces = []
        start = 0
        for p in parts:
            pieces.append(flat[start : start + p.size].reshape(p.shape))
            start += p.size
        return pieces

    total_conv_x, total_conv_bc, total_decay_log, total_step_bias, total_skip_weight, total_gated_gain = pooled(
        [
            gradient_convolve_signal,
            gradient_convolve_bc,
            gradient_log_decay,
            gradient_stepsize_bias,
            gradient_direct_weight,
            gradient_gated_norm_gain,
        ],
        ("dp",),
    )
    gain_two_wide = lax.dynamic_update_slice_in_dim(
        jnp.zeros((joined_width,), f32), gain_two_part, data_here * share, 0
    )
    total_gain_two, total_gain_three = pooled(
        [gain_two_wide, gradient_third_gain], ("dp", "tensor")
    )
    (total_gain_one,) = pooled([gain_one_part], ("dp", "tensor"))
    return (
        hidden_out,
        grad_hidden,
        grad_embed,
        total_gain_one,
        share_qkv,
        share_attn_down,
        share_attn_up,
        share_attn_out,
        total_gain_two,
        share_gate_up,
        shared_feedfwd_down_adapter,
        shared_feedfwd_up_adapter,
        share_mlp_down,
        share_linear,
        total_gain_three,
        share_in_zx,
        share_in_bc,
        share_in_dt,
        total_conv_x,
        total_conv_bc,
        total_decay_log,
        total_step_bias,
        total_skip_weight,
        total_gated_gain,
        share_out_mamba,
    )


def solution(mesh):
    in_specs = (
        P("dp", None),
        P("dp", None),
        P("dp", None),
        P("dp", None),
        P("dp", None),
        P(),
        P(None, "dp", "tensor"),
        P("dp", None),
        P(None, "dp", "tensor"),
        P("tensor", "dp"),
        P(),
        P(None, "dp", "tensor"),
        P("dp", None),
        P(None, "dp", "tensor"),
        P("tensor", "dp"),
        P("dp", None),
        P(),
        P(None, "dp", "tensor"),
        P("dp", None),
        P("dp", "tensor"),
        P(None, "tensor"),
        P(),
        P("tensor"),
        P("tensor"),
        P("tensor"),
        P("tensor"),
        P("tensor", "dp"),
    )
    out_specs = (
        P("dp", None),
        P("dp", None),
        P("dp", None),
        P(),
        P(None, "dp", "tensor"),
        P("dp", None),
        P(None, "dp", "tensor"),
        P("tensor", "dp"),
        P(),
        P(None, "dp", "tensor"),
        P("dp", None),
        P(None, "dp", "tensor"),
        P("tensor", "dp"),
        P("dp", None),
        P(),
        P(None, "dp", "tensor"),
        P("dp", None),
        P("dp", "tensor"),
        P(None, "tensor"),
        P(),
        P("tensor"),
        P("tensor"),
        P("tensor"),
        P("tensor"),
        P("tensor", "dp"),
    )
    return jax.shard_map(
        per_device, mesh=mesh, in_specs=in_specs, out_specs=out_specs, check_vma=False
    )
```
